32 devices in a mesh: frame: 4 (over y, core), row: 8 (over z, x).
Axes of the slice: x: 2, y: 2, z: 4, core: 2. Of those that a mesh axis runs over, the one named last changes fastest.
Arguments:
- latent: bfloat16 [64, 8192], P(None, ('frame', 'row')), may hold values from -6 to 6
- cond: bfloat16 [64, 8192], P(None, ('frame', 'row')), may hold values from -6 to 6
- uncond: bfloat16 [64, 8192], P(None, ('frame', 'row')), may hold values from -6 to 6
- guide_scale: float32 [1], replicated, may hold values from 3 to 7
- step_index: int32 [1], replicated, may hold values from 42 to 49
- layout_map: int32 [8192], P(('frame', 'row')), may hold values from 0 to 8191, as said below
- in_weight: bfloat16 [3, 3, 3, 16, 384], replicated, may hold values from -0.3125 to 0.3125
- in_bias: float32 [384], replicated, may hold values from -1 to 1
- first_gain: float32 [384], replicated, may hold values from 0.1 to 1.9
- first_weight: bfloat16 [3, 3, 3, 384, 384], replicated, may hold values from -0.0625 to 0.0625
- first_bias: float32 [384], replicated, may hold values from -1 to 1
- second_gain: float32 [384], replicated, may hold values from 0.1 to 1.9
- second_weight: bfloat16 [3, 3, 3, 384, 384], replicated, may hold values from -0.0625 to 0.0625
- second_bias: float32 [384], replicated, may hold values from -1 to 1
Outputs:
- features: bfloat16 [16, 16, 128, 384], P('frame', 'row')
The draws below stay inside these ranges and needn't reach their ends.
Inputs may be any that keep to these rules, and one draw needn't show every extreme that they name: `layout_map`: a permutation of the grid tokens; the 256 positions of each sequence shard hold exactly 8 tokens of every device's tile of 4 frames and 2 rows.
All inputs are finite; a program needn't handle non-finite values.
Results may differ from the reference program's by a relative error of at most 0.01.
Values may be sent and summed in bfloat16 or wider, within the bound.
A program may use at most 128 MiB of HBM per device.

```python
import jax
import jax.numpy as jnp
from jax import lax

ZC = 16
C = 384
PV = 64
FR_DEV = 4
ROW_DEV = 2
COLS = 128
STEPS = 50
FRAMES = 16
ROWS = 16
TOK_DEV = 256
TOKENS = 8192
N_ROW = 8
DEVICES = 32


def draw_layout_map(key, part):
    quota = TOK_DEV // DEVICES
    half_rows = ROW_DEV // 2
    half_cols = COLS // 2
    patch_rows = ROWS // 2
    device_ids = jnp.arange(DEVICES, dtype=jnp.int32)
    frame_of = device_ids // N_ROW
    row_of = device_ids % N_ROW
    local = jnp.arange(TOK_DEV, dtype=jnp.int32)
    local_frame = local // (half_rows * half_cols)
    local_row = local // half_cols % half_rows
    local_col = local % half_cols
    grid_ids = ((frame_of[:, None] * FR_DEV + local_frame[None, :]) * patch_rows + row_of[:, None] * half_rows + local_row[None, :]) * half_cols + local_col[None, :]
    first_key, second_key = jax.random.split(jax.random.fold_in(key, 7))
    first_perm = jax.vmap(lambda k: jax.random.permutation(k, TOK_DEV))(jax.random.split(first_key, DEVICES))
    shuffled = jnp.take_along_axis(grid_ids, first_perm, axis=1)
    by_source = shuffled.reshape(DEVICES, DEVICES, quota).transpose(1, 0, 2).reshape(DEVICES, TOK_DEV)
    second_perm = jax.vmap(lambda k: jax.random.permutation(k, TOK_DEV))(jax.random.split(second_key, DEVICES))
    return jnp.take_along_axis(by_source, second_perm, axis=1).reshape(TOKENS).astype(jnp.int32)


def shard_levels(stream_key, dims, pieces, least, high):
    def one(axis_at, parts):
        heights = jax.random.uniform(jax.random.fold_in(jax.random.fold_in(stream_key, 6), axis_at), (parts,), jnp.float32, least / len(pieces), high / len(pieces))
        return jnp.repeat(jnp.exp(heights), dims[axis_at] // parts).reshape((-1,) + (1,) * (len(dims) - axis_at - 1))

    level = one(*pieces[0])
    for cut in pieces[1:]:
        level = level * one(*cut)
    return level


def bell_draw(rng, dims, spread, limit, pieces=(), kind=jnp.bfloat16):
    values = jax.random.normal(rng, dims, jnp.float32) * spread
    if len(pieces) > 0:
        values = shard_levels(rng, dims, pieces, -0.22, 0.18) * values
    return jnp.clip(values, min=-limit, max=limit).astype(kind)


def setup_inputs(seed: int = 0) -> dict:
    key_list = jax.random.split(jax.random.key(seed), 15)
    latent = bell_draw(key_list[0], (PV, TOKENS), 1.0, 6.0, ((1, 32),))
    cond = bell_draw(key_list[1], (PV, TOKENS), 1.0, 6.0, ((1, 32),))
    uncond = bell_draw(key_list[2], (PV, TOKENS), 1.0, 6.0, ((1, 32),))
    guide_scale = jnp.clip(jax.random.uniform(key_list[3], (1,), jnp.float32, 3.0, 7.0), 3.0, 7.0)
    step_index = jax.random.randint(key_list[4], (1,), STEPS - 8, STEPS).astype(jnp.int32)
    layout_map = draw_layout_map(jax.random.fold_in(key_list[14], 71), 0)
    in_weight = bell_draw(key_list[6], (3, 3, 3, ZC, C), (27 * ZC) ** -0.5, 0.3125)
    in_bias = bell_draw(key_list[7], (C,), 0.3, 1.0, (), jnp.float32)
    first_gain = jnp.clip(1.0 + 0.18 * jax.random.normal(key_list[8], (C,), jnp.float32), 0.1, 1.9)
    first_weight = bell_draw(key_list[9], (3, 3, 3, C, C), (27 * C) ** -0.5, 0.0625)
    first_bias = bell_draw(key_list[10], (C,), 0.3, 1.0, (), jnp.float32)
    second_gain = jnp.clip(1.0 + 0.18 * jax.random.normal(key_list[11], (C,), jnp.float32), 0.1, 1.9)
    second_weight = bell_draw(key_list[12], (3, 3, 3, C, C), (27 * C) ** -0.5, 0.0625)
    second_bias = bell_draw(key_list[13], (C,), 0.3, 1.0, (), jnp.float32)
    return {"latent": latent, "cond": cond, "uncond": uncond, "guide_scale": guide_scale, "step_index": step_index, "layout_map": layout_map, "in_weight": in_weight, "in_bias": in_bias, "first_gain": first_gain, "first_weight": first_weight, "first_bias": first_bias, "second_gain": second_gain, "second_weight": second_weight, "second_bias": second_bias}


SHIFT_FACTOR = 5.0

def sigma_at(index):
    level = 1.0 - index.astype(jnp.float32) / STEPS
    return SHIFT_FACTOR * level / (1.0 + (SHIFT_FACTOR - 1.0) * level)

def causal_conv(field, weight, bias):
    out = lax.conv_general_dilated(field.astype(jnp.float32)[None], weight.astype(jnp.float32), (1, 1, 1), ((2, 0), (1, 1), (1, 1)), dimension_numbers=('NDHWC', 'DHWIO', 'NDHWC'), precision=lax.Precision.HIGHEST)[0]
    return out + bias

def channel_norm(value, gain):
    return value * lax.rsqrt(lax.optimization_barrier(jnp.mean(value * value, axis=-1, keepdims=True)) + 1e-06) * gain

def reference(latent, cond, uncond, guide_scale, step_index, layout_map, in_weight, in_bias, first_gain, first_weight, first_bias, second_gain, second_weight, second_bias):
    delta = sigma_at(step_index + 1) - sigma_at(step_index)
    base = uncond.astype(jnp.float32)
    moved = (latent.astype(jnp.float32) + delta * (base + guide_scale * (cond.astype(jnp.float32) - base))).astype(jnp.bfloat16)
    placed = jnp.zeros((TOKENS, PV), jnp.bfloat16).at[layout_map].set(moved.T)
    grid = placed.reshape(FRAMES, ROWS // 2, COLS // 2, 2, 2, ZC).transpose(0, 1, 3, 2, 4, 5).reshape(FRAMES, ROWS, COLS, ZC)
    hidden = causal_conv(grid, in_weight, in_bias).astype(jnp.bfloat16)
    act_one = jax.nn.silu(channel_norm(hidden.astype(jnp.float32), first_gain)).astype(jnp.bfloat16)
    inner = causal_conv(act_one, first_weight, first_bias)
    act_two = jax.nn.silu(channel_norm(inner, second_gain)).astype(jnp.bfloat16)
    result = hidden.astype(jnp.float32) + causal_conv(act_two, second_weight, second_bias)
    return result.astype(jnp.bfloat16)
```

```python
import jax
import jax.numpy as jnp
from jax import lax
from jax.experimental import pallas as pl
from jax.experimental.pallas import tpu as pltpu
from jax.sharding import PartitionSpec as P

ZC = 16
FR_DEV = 4
ROW_DEV = 2
COLS = 128
STEPS = 50
C = 384


SHIFT_FACTOR = 5.0
BF = jnp.bfloat16
F32 = jnp.float32
MESH = pl.DeviceIdType.MESH


def neighbour(block, axis, distance):
    devices = range(lax.axis_size(axis))
    route = [(i - distance, i) for i in devices if i - distance in devices]
    return lax.ppermute(block, axis, route)


def sigma_at(index):
    level = 1.0 - index.astype(jnp.float32) / STEPS
    return SHIFT_FACTOR * level / (1.0 + (SHIFT_FACTOR - 1.0) * level)


def advance(latent, cond, uncond, guide_scale, delta):
    base = uncond.astype(jnp.float32)
    return (
        latent.astype(jnp.float32)
        + delta * (base + guide_scale * (cond.astype(jnp.float32) - base))
    ).astype(jnp.bfloat16)


def norm_silu(value, gain):
    scale = lax.rsqrt(jnp.mean(value * value, axis=-1, keepdims=True) + 1e-06)
    v = value * scale * gain
    return v / (1.0 + jnp.exp(-v))


def col_sum(acc):
    line = lax.broadcasted_iota(jnp.int32, (COLS, C), 0)
    left = jnp.where(line == 0, 0.0, pltpu.roll(acc[:, :C], 1, 0))
    right = jnp.where(line == COLS - 1, 0.0, pltpu.roll(acc[:, 2 * C :], COLS - 1, 0))
    return acc[:, C : 2 * C] + left + right


def taps(w, kt, krs):
    return jnp.concatenate(
        [jnp.concatenate([w[kt, kr, kc] for kc in range(3)], 1) for kr in krs], 0
    )


def block_kernel(
    g_ref, wi_ref, bi_ref, g1_ref, w1_hbm, b1_ref, g2_ref, w2_hbm, b2_ref, out_ref,
    z, act1, act2, hidden, acc, w1, w2, w_sem, send_sem, recv_sem,
):
    fi = lax.axis_index("frame")
    ri = lax.axis_index("row")
    n_frame = lax.axis_size("frame")
    n_row = lax.axis_size("row")
    has_up = ri > 0
    has_down = ri < n_row - 1
    has_prev = fi > 0
    has_next = fi < n_frame - 1
    up = (fi, jnp.maximum(ri - 1, 0))
    down = (fi, jnp.minimum(ri + 1, n_row - 1))
    prev = (jnp.maximum(fi - 1, 0), ri)
    nxt = (jnp.minimum(fi + 1, n_frame - 1), ri)

    w1_copy = pltpu.make_async_copy(w1_hbm, w1, w_sem.at[0])
    w2_copy = pltpu.make_async_copy(w2_hbm, w2, w_sem.at[1])
    w1_copy.start()
    w2_copy.start()

    barrier = pltpu.get_barrier_semaphore()
    count = jnp.int32(0)
    for exists, who in ((has_up, up), (has_down, down), (has_prev, prev), (has_next, nxt)):
        @pl.when(exists)
        def _(who=who):
            pl.semaphore_signal(barrier, inc=1, device_id=who, device_id_type=MESH)
        count = count + jnp.where(exists, 1, 0)

    @pl.when(jnp.logical_not(has_up))
    def _():
        act2[:, 0] = jnp.zeros((6, COLS, C), BF)

    @pl.when(jnp.logical_not(has_down))
    def _():
        act2[:, 3] = jnp.zeros((6, COLS, C), BF)

    @pl.when(jnp.logical_not(has_prev))
    def _():
        act2[0:2] = jnp.zeros((2, 4, COLS, C), BF)

    lane = lax.broadcasted_iota(jnp.int32, (6 * ZC, COLS), 1)

    def spread(t, _):
        mid = g_ref[t].reshape(6 * ZC, COLS).astype(F32)
        left = jnp.where(lane == 0, 0.0, pltpu.roll(mid, 1, 1))
        right = jnp.where(lane == COLS - 1, 0.0, pltpu.roll(mid, COLS - 1, 1))
        for kc, part in enumerate((left, mid, right)):
            z[t, :, kc * ZC : (kc + 1) * ZC] = part.astype(BF).reshape(6, ZC, COLS)
        return 0

    lax.fori_loop(0, 8, spread, 0)

    def entry(t, _):
        cells = jnp.concatenate(
            [
                jnp.concatenate(
                    [z[t + kt, r : r + 3].reshape(9 * ZC, COLS) for kt in range(3)], 0
                )
                for r in range(4)
            ],
            1,
        )
        value = lax.dot_general(
            cells, wi_ref[...], (((0,), (0,)), ((), ())), preferred_element_type=F32
        )
        value = (value + bi_ref[...]).astype(BF)
        early = jnp.logical_and(t < 2, jnp.logical_not(has_prev))
        for r in range(4):
            cell = value[r * COLS : (r + 1) * COLS]
            if r in (1, 2):
                hidden[t, r - 1] = cell
            act = norm_silu(cell.astype(F32), g1_ref[...])
            outside = early
            if r == 0:
                outside = jnp.logical_or(early, jnp.logical_not(has_up))
            if r == 3:
                outside = jnp.logical_or(early, jnp.logical_not(has_down))
            act1[t, r] = jnp.where(outside, 0.0, act).astype(BF)
        return 0

    lax.fori_loop(0, 6, entry, 0)

    w1_copy.wait()
    pl.semaphore_wait(barrier, count)

    def send(slot, src, dst, who):
        return pltpu.make_async_remote_copy(
            src_ref=src,
            dst_ref=dst,
            send_sem=send_sem.at[slot],
            recv_sem=recv_sem.at[slot],
            device_id=who,
            device_id_type=MESH,
        )

    up_a = send(0, act2.at[4:6, 1], act2.at[4:6, 3], up)
    down_a = send(1, act2.at[4:6, 2], act2.at[4:6, 0], down)
    own = send(2, act2.at[4:6, 1:3], act2.at[0:2, 1:3], nxt)
    up_b = send(3, act2.at[2:4, 1], act2.at[2:4, 3], up)
    down_b = send(4, act2.at[2:4, 2], act2.at[2:4, 0], down)
    fore_top = send(5, act2.at[4:6, 0], act2.at[0:2, 0], nxt)
    fore_low = send(6, act2.at[4:6, 3], act2.at[0:2, 3], nxt)
    top_next = jnp.logical_and(has_up, has_next)
    low_next = jnp.logical_and(has_down, has_next)
    top_prev = jnp.logical_and(has_up, has_prev)
    low_prev = jnp.logical_and(has_down, has_prev)

    for t0 in (2, 0):
        def first(kt, _, t0=t0):
            rows = act1[pl.ds(t0 + kt, 2)]
            cells = jnp.concatenate([rows[:, kr : kr + 2] for kr in range(3)], -1)
            part = jnp.dot(
                cells.reshape(4 * COLS, 3 * C), taps(w1, kt, (0, 1, 2)),
                preferred_element_type=F32,
            ).reshape(2, 2, COLS, 3 * C)

            @pl.when(kt == 0)
            def _():
                acc[t0 : t0 + 2] = part

            @pl.when(kt > 0)
            def _():
                acc[t0 : t0 + 2] += part

            return 0

        lax.fori_loop(0, 3, first, 0)

        def close(i, _, t0=t0):
            t, r = t0 + i // 2, i % 2
            inner = col_sum(acc[t, r]) + b1_ref[...]
            act2[2 + t, 1 + r] = norm_silu(inner, g2_ref[...]).astype(BF)
            return 0

        lax.fori_loop(0, 4, close, 0)
        pairs = ((has_up, up_a), (has_down, down_a), (has_next, own))
        if t0 == 0:
            pairs = ((has_up, up_b), (has_down, down_b))
        for exists, copy in pairs:
            @pl.when(exists)
            def _(copy=copy):
                copy.start()

    w2_copy.wait()

    def inside(r):
        for kt in (2, 1, 0):
            t = 2 - kt
            n = 4 - t
            cells = jnp.concatenate([act2[2 : 2 + n, 1], act2[2 : 2 + n, 2]], -1)
            part = jnp.dot(
                cells.reshape(n * COLS, 2 * C), taps(w2, kt, (1 - r, 2 - r)),
                preferred_element_type=F32,
            ).reshape(n, COLS, 3 * C)
            if kt == 2:
                acc[:, r] = part
            else:
                acc[t:, r] += part

    inside(0)
    for arrived, copy, ahead, onward in (
        (has_down, up_a, low_next, fore_low),
        (has_up, down_a, top_next, fore_top),
    ):
        @pl.when(arrived)
        def _(copy=copy):
            copy.wait_recv()

        @pl.when(ahead)
        def _(onward=onward):
            onward.start()

    inside(1)

    @pl.when(has_prev)
    def _():
        own.wait_recv()

    for r in range(2):
        for kt, n in ((0, 2), (1, 1)):
            cells = jnp.concatenate([act2[kt : kt + n, 1], act2[kt : kt + n, 2]], -1)
            acc[:n, r] += jnp.dot(
                cells.reshape(n * COLS, 2 * C), taps(w2, kt, (1 - r, 2 - r)),
                preferred_element_type=F32,
            ).reshape(n, COLS, 3 * C)

    for arrived, copy in (
        (top_prev, fore_top), (low_prev, fore_low), (has_down, up_b), (has_up, down_b)
    ):
        @pl.when(arrived)
        def _(copy=copy):
            copy.wait_recv()

    for r, row, kr in ((0, 0, 0), (1, 3, 2)):
        cells = jnp.concatenate([act2[kt : kt + 4, row] for kt in range(3)], -1)
        weight = jnp.concatenate([taps(w2, kt, (kr,)) for kt in range(3)], 0)
        acc[:, r] += jnp.dot(
            cells.reshape(4 * COLS, 3 * C), weight, preferred_element_type=F32
        ).reshape(4, COLS, 3 * C)

    def finish(i, _):
        t, r = i // 2, i % 2
        total = col_sum(acc[t, r]) + b2_ref[...]
        out_ref[t, r] = (hidden[t + 2, r].astype(F32) + total).astype(BF)
        return 0

    lax.fori_loop(0, 8, finish, 0)

    for exists, copy in (
        (has_up, up_a), (has_down, down_a), (has_next, own), (has_up, up_b),
        (has_down, down_b), (top_next, fore_top), (low_next, fore_low),
    ):
        @pl.when(exists)
        def _(copy=copy):
            copy.wait_send()


def residual(grid, wi, bi, g1, w1, b1, g2, w2, b2):
    vmem = pl.BlockSpec(memory_space=pltpu.VMEM)
    hbm = pl.BlockSpec(memory_space=pl.ANY)
    return pl.pallas_call(
        block_kernel,
        out_shape=jax.ShapeDtypeStruct((FR_DEV, ROW_DEV, COLS, C), BF),
        in_specs=[vmem, vmem, vmem, vmem, hbm, vmem, vmem, hbm, vmem],
        out_specs=vmem,
        scratch_shapes=[
            pltpu.VMEM((8, 6, 3 * ZC, COLS), BF),
            pltpu.VMEM((6, 4, COLS, C), BF),
            pltpu.VMEM((6, 4, COLS, C), BF),
            pltpu.VMEM((6, 2, COLS, C), BF),
            pltpu.VMEM((4, 2, COLS, 3 * C), F32),
            pltpu.VMEM((3, 3, 3, C, C), BF),
            pltpu.VMEM((3, 3, 3, C, C), BF),
            pltpu.SemaphoreType.DMA((2,)),
            pltpu.SemaphoreType.DMA((7,)),
            pltpu.SemaphoreType.DMA((7,)),
        ],
        compiler_params=pltpu.CompilerParams(
            collective_id=0, has_side_effects=True, vmem_limit_bytes=60 * 1024 * 1024
        ),
        name="residual",
    )(grid, wi, bi, g1, w1, b1, g2, w2, b2)


def local(
    latent,
    cond,
    uncond,
    guide_scale,
    step_index,
    layout_map,
    in_weight,
    in_bias,
    first_gain,
    first_weight,
    first_bias,
    second_gain,
    second_weight,
    second_bias,
):
    n_frame = lax.axis_size("frame")
    n_row = lax.axis_size("row")
    devices = n_frame * n_row
    values, tok_dev = latent.shape
    quota = tok_dev // devices
    frames = FR_DEV
    rows = ROW_DEV
    cols = COLS
    half_rows = rows // 2
    half_cols = cols // 2
    patch_rows = half_rows * n_row
    delta = sigma_at(step_index + 1) - sigma_at(step_index)
    frame_at = layout_map // (patch_rows * half_cols)
    row_at = layout_map // half_cols % patch_rows
    target = frame_at // frames * n_row + row_at // half_rows
    place = frame_at % frames * half_cols + layout_map % half_cols
    moved = advance(latent, cond, uncond, guide_scale, delta)
    hit = (target[:, None] == jnp.arange(devices)[None, :]).astype(BF)
    before = (jnp.arange(tok_dev)[:, None] > jnp.arange(tok_dev)[None, :]).astype(BF)
    ahead = jnp.dot(before, hit, preferred_element_type=F32)
    rank = jnp.sum(ahead * hit.astype(F32), axis=1).astype(jnp.int32)
    slot = target * quota + rank
    sort = (slot[None, :] == jnp.arange(tok_dev)[:, None]).astype(BF)
    load = jnp.concatenate(
        [moved, place[None].astype(BF), jnp.zeros((127 - values, tok_dev), BF)], 0
    )
    payload = lax.dot_general(
        sort, load, (((1,), (1,)), ((), ())), preferred_element_type=F32
    ).astype(BF)
    got = lax.all_to_all(
        payload.reshape(devices, quota, 128), ("frame", "row"), split_axis=0, concat_axis=0,
        tiled=True,
    ).reshape(tok_dev, 128)
    where = got[:, values].astype(jnp.int32)
    cell = jnp.arange(frames * cols)
    spot = cell // cols * half_cols + cell % cols // 2
    field = 0.0
    tokens = got[:, :values].reshape(tok_dev, 2, 2, ZC)
    for b in range(2):
        chosen = (where[:, None] == jnp.where(cell % 2 == b, spot, -1)[None, :]).astype(BF)
        field = field + lax.dot_general(
            tokens[:, :, b].reshape(tok_dev, 2 * ZC), chosen, (((0,), (0,)), ((), ())),
            preferred_element_type=F32,
        )
    grid = field.astype(BF).reshape(2, ZC, frames, cols).transpose(2, 0, 1, 3)
    grid = jnp.concatenate([neighbour(grid, "frame", 1), grid], 0)
    grid = jnp.concatenate([neighbour(grid, "row", 1), grid, neighbour(grid, "row", -1)], 1)
    return residual(
        grid,
        in_weight.reshape(27 * ZC, C),
        in_bias[None],
        first_gain[None],
        first_weight,
        first_bias[None],
        second_gain[None],
        second_weight,
        second_bias[None],
    )


def solution(mesh):
    in_specs = (
        P(None, ("frame", "row")),
        P(None, ("frame", "row")),
        P(None, ("frame", "row")),
        P(),
        P(),
        P(("frame", "row")),
        P(),
        P(),
        P(),
        P(),
        P(),
        P(),
        P(),
        P(),
    )
    out_specs = P("frame", "row", None, None)
    return jax.shard_map(local, mesh=mesh, in_specs=in_specs, out_specs=out_specs, check_vma=False)
```
